32 devices in a mesh: section: 4 (over x, core), expert: 8 (over z, y).
Axes of the slice: x: 2, y: 2, z: 4, core: 2. Of those that a mesh axis runs over, the one named last changes fastest.
Arguments:
- sent_acts: bfloat16 [4, 512, 2048], P('section', 'expert'), may hold values from -6 to 6
- stash: bfloat16 [4, 512, 2048], P('section', 'expert'), may hold values from -6 to 6
- cotangents: bfloat16 [4, 512, 2048], P('section', 'expert'), may hold values from -6 to 6
- norm_gain: bfloat16 [4, 2048], P('section'), may hold values from 0.5 to 1.5
- w_gate: bfloat16 [4, 16, 2048, 768], P('section', 'expert'), may hold values from -0.125 to 0.125
- w_up: bfloat16 [4, 16, 2048, 768], P('section', 'expert'), may hold values from -0.125 to 0.125
- w_down: bfloat16 [4, 16, 768, 2048], P('section', 'expert'), may hold values from -0.21875 to 0.21875
- routes_next: int32 [4, 512, 8], P('section', 'expert'), may hold values from 0 to 15, all different within a row; in each aligned block of 64 rows (0 to 63, 64 to 127, ..., all dimensions but the last counted through in order) at most 48 rows name the same one
- gates_next: bfloat16 [4, 512, 8], P('section', 'expert'), may hold values from 0.049804688 to 0.5
- routes_prev: int32 [4, 512, 8], P('section', 'expert'), may hold values from 0 to 15, all different within a row; in each aligned block of 64 rows (0 to 63, 64 to 127, ..., all dimensions but the last counted through in order) at most 48 rows name the same one
- gates_prev: bfloat16 [4, 512, 8], P('section', 'expert'), may hold values from 0.049804688 to 0.5
Outputs:
- fwd_out: bfloat16 [4, 512, 2048], P('section', 'expert')
- bwd_out: bfloat16 [4, 512, 2048], P('section', 'expert')
- gate_grad: bfloat16 [4, 512, 8], P('section', 'expert')
- grad_w_gate: bfloat16 [4, 16, 2048, 768], P('section', 'expert')
- grad_w_up: bfloat16 [4, 16, 2048, 768], P('section', 'expert')
- grad_w_down: bfloat16 [4, 16, 768, 2048], P('section', 'expert')
The draws below stay inside these ranges and needn't reach their ends.
Inputs may be any that keep to these rules, and one draw needn't show every extreme that they name: `routes_next`: each row names 8 different experts. At most 48 of the 64 tokens of one device choose one expert, and in some device's tokens some expert is chosen by exactly 48. `routes_prev`: each row names 8 different experts. At most 48 of the 64 tokens of one device choose one expert, and in some device's tokens some expert is chosen by exactly 48.
All inputs are finite; a program needn't handle non-finite values.
Results may differ from the reference program's by a relative error of at most 0.008.
Values may be sent and summed in bfloat16 or wider, within the bound.
A program may use at most 128 MiB of HBM per device.

```python
import math
import jax
import jax.numpy as jnp
import numpy as np
from jax import lax

D = 2048
FF = 768
EXPERTS = 16
TOP = 8
TOK_DEV = 64
SECTIONS = 4
TOKENS = 512
CAP = 48
N_EXPERT = 8


def level_of(own_key, dims, split, low, top_value):
    def one(dim, blocks):
        heights = jax.random.uniform(jax.random.fold_in(jax.random.fold_in(own_key, 6), dim), (blocks,), jnp.float32, low / len(split), top_value / len(split))
        return jnp.repeat(jnp.exp(heights), dims[dim] // blocks).reshape((-1,) + (1,) * (len(dims) - dim - 1))

    gain = one(*split[0])
    for cut in split[1:]:
        gain = gain * one(*cut)
    return gain


def routed_block(stream_key, own, number, rows, number_of, top, limit, lean):
    ranking = jax.random.permutation(stream_key, number_of)
    packed, common = portions_of(number_of, rows * top, limit, lean, True), portions_of(number_of, rows * top, limit, lean, False)
    places = jnp.arange(number_of)

    def named(sizes, offset_by):
        used = int((sizes > 0).sum())
        fixed = max(1, used // 4)
        shifted = fixed + (places - fixed + offset_by * (used - fixed)) % max(1, number_of - fixed)
        return jnp.zeros((number_of,), jnp.int32).at[ranking[jnp.where(places < fixed, places, shifted)]].set(jnp.asarray(sizes, jnp.int32))

    sizes = jnp.where(number % 4 == 0, named(packed, number // 4), named(common, number - number // 4 - 1))
    mixed = jax.random.permutation(jax.random.fold_in(own, 3), number_of)
    donor, taker = mixed[0:number_of // 2 * 2:2], mixed[1:number_of // 2 * 2:2]
    slack = jnp.minimum(sizes[donor] - 1, limit - sizes[taker]) // 2
    slack = jnp.where((donor == ranking[0]) | (taker == ranking[0]) | (sizes[taker] == 0), 0, jnp.maximum(slack, 0))
    shifted = jax.random.randint(jax.random.fold_in(own, 4), (number_of // 2,), 0, 1 << 20) % (slack + 1)
    sizes = sizes.at[donor].add(-shifted).at[taker].add(shifted)
    items = jnp.searchsorted(jnp.cumsum(sizes), jnp.arange(rows * top), side="right").astype(jnp.int32)
    table = items.reshape(top, rows).T
    table = table[jax.random.permutation(jax.random.fold_in(own, 1), rows)]
    offset_by = jax.random.randint(jax.random.fold_in(own, 2), (rows, 1), 0, top)
    return jnp.take_along_axis(table, (jnp.arange(top)[None, :] + offset_by) % top, axis=1)


def portions_of(number_of, total, reach, skew, full):
    loads = [(1 << 20) // math.isqrt(standing ** skew) + 1 for standing in range(1, number_of + 1)]
    largest = reach if full else min(reach, max(-(-total // number_of), total * loads[0] // sum(loads)))
    least = 1 if total - largest >= number_of - 1 else 0
    given, surplus = [largest] + [least] * (number_of - 1), total - largest - least * (number_of - 1)
    while surplus > 0:
        movable = [i for i in range(1, number_of) if given[i] < largest] or [i for i in range(1, number_of) if given[i] < reach]
        mass, left = sum([loads[i] for i in movable]), surplus
        for i in movable:
            more = min(reach - given[i], max(1, left * loads[i] // mass), surplus)
            given[i] = given[i] + more
            surplus = surplus - more
    return np.array(given)


def noise(own_key, shape, spread, bound, cuts=(), held_as=jnp.bfloat16):
    entries = jax.random.normal(own_key, shape, jnp.float32) * spread
    if len(cuts) > 0:
        entries = level_of(own_key, shape, cuts, -0.22, 0.18) * entries
    return jnp.clip(entries, min=-bound, max=bound).astype(held_as)


def setup_inputs(seed: int = 0) -> dict:
    key_list = jax.random.split(jax.random.key(seed), 12)
    sent_acts = noise(key_list[0], (SECTIONS, TOKENS, D), 1.0, 6.0, ((0, 4), (1, 8)))
    stash = noise(key_list[1], (SECTIONS, TOKENS, D), 1.0, 6.0, ((0, 4), (1, 8)))
    cotangents = noise(key_list[2], (SECTIONS, TOKENS, D), 1.0, 6.0, ((0, 4), (1, 8)))
    norm_gain = jnp.clip(1.0 + 0.1 * jax.random.normal(key_list[3], (SECTIONS, D), jnp.float32), 0.5, 1.5).astype(jnp.bfloat16)
    w_gate = noise(key_list[4], (SECTIONS, EXPERTS, D, FF), D ** -0.5, 0.125, ((0, 4), (1, 8)))
    w_up = noise(key_list[5], (SECTIONS, EXPERTS, D, FF), D ** -0.5, 0.125, ((0, 4), (1, 8)))
    w_down = noise(key_list[6], (SECTIONS, EXPERTS, FF, D), FF ** -0.5, 0.21875, ((0, 4), (1, 8)))
    routes_next_keys = jax.random.split(jax.random.fold_in(key_list[7], 1), SECTIONS * TOKENS // TOK_DEV)
    routes_next_turns = jax.random.permutation(jax.random.fold_in(key_list[7], 3), SECTIONS * TOKENS // TOK_DEV)
    routes_next = jax.vmap(lambda own, number: routed_block(jax.random.fold_in(key_list[7], 2), own, number, TOK_DEV, EXPERTS, TOP, CAP, 2))(routes_next_keys, routes_next_turns).reshape((SECTIONS, TOKENS, TOP))
    gates_next = jnp.clip(jnp.exp(math.log(0.5) - 2.306499 * jax.random.uniform(key_list[8], (SECTIONS, TOKENS, TOP), jnp.float32) ** level_of(key_list[8], (SECTIONS, TOKENS, TOP), ((0, 4), (1, 8)), -0.2, 0.2)), 0.049804688, 0.5).astype(jnp.bfloat16)
    routes_prev_keys = jax.random.split(jax.random.fold_in(key_list[9], 1), SECTIONS * TOKENS // TOK_DEV)
    routes_prev_turns = jax.random.permutation(jax.random.fold_in(key_list[9], 3), SECTIONS * TOKENS // TOK_DEV)
    routes_prev = jax.vmap(lambda own, number: routed_block(jax.random.fold_in(key_list[9], 2), own, number, TOK_DEV, EXPERTS, TOP, CAP, 2))(routes_prev_keys, routes_prev_turns).reshape((SECTIONS, TOKENS, TOP))
    gates_prev = jnp.clip(jnp.exp(math.log(0.5) - 2.306499 * jax.random.uniform(key_list[10], (SECTIONS, TOKENS, TOP), jnp.float32) ** level_of(key_list[10], (SECTIONS, TOKENS, TOP), ((0, 4), (1, 8)), -0.2, 0.2)), 0.049804688, 0.5).astype(jnp.bfloat16)
    return {"sent_acts": sent_acts, "stash": stash, "cotangents": cotangents, "norm_gain": norm_gain, "w_gate": w_gate, "w_up": w_up, "w_down": w_down, "routes_next": routes_next, "gates_next": gates_next, "routes_prev": routes_prev, "gates_prev": gates_prev}


EPS = 1e-06

def apply_rms_norm(rows, norm_scale_weight):
    value_entries = rows.astype(jnp.float32)
    inverse_root_scale = lax.rsqrt(lax.optimization_barrier(jnp.mean(value_entries * value_entries, axis=-1, keepdims=True)) + EPS)
    unit_rows = value_entries * inverse_root_scale
    normalized_rows = (unit_rows * norm_scale_weight.astype(jnp.float32)).astype(jnp.bfloat16)
    return (normalized_rows, unit_rows, inverse_root_scale)

def place_slots(routes):
    flat = routes.reshape(-1).astype(jnp.int32)
    onehot = (flat[:, None] == jnp.arange(EXPERTS, dtype=jnp.int32)[None, :]).astype(jnp.int32)
    before = jnp.cumsum(onehot, axis=0) - onehot
    slot = lax.optimization_barrier(jnp.sum(before * onehot, axis=1)).astype(jnp.int32)
    return (flat, slot)

def dispatch(rows, flat, slot):

    def one_block(block_rows, block_flat, block_slot):
        buffer = jnp.zeros((EXPERTS, CAP) + block_rows.shape[1:], block_rows.dtype)
        return buffer.at[block_flat, block_slot].set(block_rows)
    buffers = jax.vmap(one_block)(rows, flat, slot)
    return jnp.swapaxes(buffers, 0, 1)

def collect(buffers, flat, slot):
    per_block = jnp.swapaxes(buffers, 0, 1)
    return jax.vmap(lambda block, block_flat, block_slot: block[block_flat, block_slot])(per_block, flat, slot)

def expert_forward(args):
    rows, weight_gate, weight_up, weight_down = args
    pre_gate = jnp.dot(rows, weight_gate, preferred_element_type=jnp.float32)
    pre_up = jnp.dot(rows, weight_up, preferred_element_type=jnp.float32)
    hidden = (jax.nn.silu(pre_gate) * pre_up).astype(jnp.bfloat16)
    return jnp.dot(hidden, weight_down, preferred_element_type=jnp.float32).astype(jnp.bfloat16)

def expert_backward(args):
    rows, out_grad, weight_gate, weight_up, weight_down = args
    pre_gate = jnp.dot(rows, weight_gate, preferred_element_type=jnp.float32)
    pre_up = jnp.dot(rows, weight_up, preferred_element_type=jnp.float32)
    sigma = jax.nn.sigmoid(pre_gate)
    active = pre_gate * sigma
    hidden = (active * pre_up).astype(jnp.bfloat16)
    expert_out = jnp.dot(hidden, weight_down, preferred_element_type=jnp.float32).astype(jnp.bfloat16)
    d_hidden = jnp.dot(out_grad, weight_down.T, preferred_element_type=jnp.float32)
    d_gate = (d_hidden * pre_up * sigma * (1.0 + pre_gate * (1.0 - sigma))).astype(jnp.bfloat16)
    d_up = (d_hidden * active).astype(jnp.bfloat16)
    row_grad = (jnp.dot(d_gate, weight_gate.T, preferred_element_type=jnp.float32) + jnp.dot(d_up, weight_up.T, preferred_element_type=jnp.float32)).astype(jnp.bfloat16)
    grad_gate = jnp.dot(rows.T, d_gate, preferred_element_type=jnp.float32).astype(jnp.bfloat16)
    grad_up = jnp.dot(rows.T, d_up, preferred_element_type=jnp.float32).astype(jnp.bfloat16)
    grad_down = jnp.dot(hidden.T, out_grad, preferred_element_type=jnp.float32).astype(jnp.bfloat16)
    return (expert_out, row_grad, grad_gate, grad_up, grad_down)

def reference(sent_acts, stash, cotangents, norm_gain, w_gate, w_up, w_down, routes_next, gates_next, routes_prev, gates_prev):
    fwd_list, bwd_list, gate_list, wg_list, wu_list, wd_list = ([], [], [], [], [], [])
    for section_index in range(SECTIONS):
        norm_scale_weight = norm_gain[section_index]
        weight_gate, weight_up, weight_down = (w_gate[section_index], w_up[section_index], w_down[section_index])
        arrived = sent_acts[(section_index - 1) % SECTIONS]
        normalized_rows, _, _ = apply_rms_norm(arrived, norm_scale_weight)
        flat, slot = jax.vmap(place_slots)(routes_next[section_index].reshape(N_EXPERT, TOK_DEV, TOP))
        rows = jnp.repeat(normalized_rows, TOP, axis=0).reshape(N_EXPERT, TOK_DEV * TOP, D)
        buffers = dispatch(rows, flat, slot).reshape(EXPERTS, N_EXPERT * CAP, D)
        outputs = lax.map(expert_forward, (buffers, weight_gate, weight_up, weight_down))
        picked = collect(outputs.reshape(EXPERTS, N_EXPERT, CAP, D), flat, slot).reshape(TOKENS, TOP, D)
        mixed = lax.optimization_barrier(jnp.sum(gates_next[section_index].astype(jnp.float32)[..., None] * picked.astype(jnp.float32), axis=1))
        fwd_list.append((arrived.astype(jnp.float32) + mixed).astype(jnp.bfloat16))
        received_rows = cotangents[(section_index + 1) % SECTIONS]
        previous_normalized_rows, unit_rows, inverse_root_scale = apply_rms_norm(stash[section_index], norm_scale_weight)
        flat_prev, slot_prev = jax.vmap(place_slots)(routes_prev[section_index].reshape(N_EXPERT, TOK_DEV, TOP))
        rows_prev = jnp.repeat(previous_normalized_rows, TOP, axis=0).reshape(N_EXPERT, TOK_DEV * TOP, D)
        out_grad = (gates_prev[section_index].astype(jnp.float32)[..., None] * received_rows.astype(jnp.float32)[:, None, :]).astype(jnp.bfloat16)
        out_grad = out_grad.reshape(N_EXPERT, TOK_DEV * TOP, D)
        row_buffers = dispatch(rows_prev, flat_prev, slot_prev).reshape(EXPERTS, N_EXPERT * CAP, D)
        grad_buffers = dispatch(out_grad, flat_prev, slot_prev).reshape(EXPERTS, N_EXPERT * CAP, D)
        expert_out, row_grad, grad_gate, grad_up, grad_down = lax.map(expert_backward, (row_buffers, grad_buffers, weight_gate, weight_up, weight_down))
        out_pick = collect(expert_out.reshape(EXPERTS, N_EXPERT, CAP, D), flat_prev, slot_prev).reshape(TOKENS, TOP, D)
        selected_gradient = collect(row_grad.reshape(EXPERTS, N_EXPERT, CAP, D), flat_prev, slot_prev).reshape(TOKENS, TOP, D)
        gate_list.append(lax.optimization_barrier(jnp.sum(out_pick.astype(jnp.float32) * received_rows.astype(jnp.float32)[:, None, :], axis=-1)).astype(jnp.bfloat16))
        normalized_gradient = lax.optimization_barrier(jnp.sum(selected_gradient.astype(jnp.float32), axis=1)) * norm_scale_weight.astype(jnp.float32)
        backward_result = received_rows.astype(jnp.float32) + inverse_root_scale * (normalized_gradient - unit_rows * lax.optimization_barrier(jnp.mean(normalized_gradient * unit_rows, axis=-1, keepdims=True)))
        bwd_list.append(backward_result.astype(jnp.bfloat16))
        wg_list.append(grad_gate)
        wu_list.append(grad_up)
        wd_list.append(grad_down)
    return (jnp.stack(fwd_list), jnp.stack(bwd_list), jnp.stack(gate_list), jnp.stack(wg_list), jnp.stack(wu_list), jnp.stack(wd_list))
```

```python
import jax
import jax.numpy as jnp
from jax import lax
from jax.sharding import PartitionSpec as P

EPS = 1e-06
F32 = jnp.float32
BF16 = jnp.bfloat16


def shifted(array, axis, by):
    count = lax.axis_size(axis)
    return lax.ppermute(array, axis, [(i, (i + by) % count) for i in range(count)])


def apply_rms_norm(rows, gain):
    values = rows.astype(F32)
    scale = lax.rsqrt(jnp.mean(values * values, axis=-1, keepdims=True) + EPS)
    unit = values * scale
    return (unit * gain).astype(BF16), unit, scale


def dense_gates(routes, gates, experts_all):
    hit = routes[:, :, None] == jnp.arange(experts_all, dtype=jnp.int32)
    return jnp.sum(jnp.where(hit, gates.astype(F32)[:, :, None], 0.0), axis=1).astype(BF16)


def dot(a, b, ca, cb):
    return lax.dot_general(a, b, (((ca,), (cb,)), ((), ())), preferred_element_type=F32)


def gathered(array):
    return lax.all_gather(array, "expert", axis=0, tiled=True)


def per_device(
    sent_acts,
    stash,
    cotangents,
    norm_gain,
    w_gate,
    w_up,
    w_down,
    routes_next,
    gates_next,
    routes_prev,
    gates_prev,
):
    owners = lax.axis_size("expert")
    me = lax.axis_index("expert")
    gain = norm_gain[0].astype(F32)
    wg, wu, wd = w_gate[0], w_up[0], w_down[0]
    local, width, hidden_units = wg.shape
    experts_all = local * owners
    tokens = stash.shape[1]

    dense = jnp.concatenate(
        [
            dense_gates(routes_next[0], gates_next[0], experts_all),
            dense_gates(routes_prev[0], gates_prev[0], experts_all),
        ],
        axis=1,
    )
    cot = shifted(cotangents, "section", -1)[0]
    arrived = shifted(sent_acts, "section", 1)[0]
    prev_rows, unit_rows, scale = apply_rms_norm(stash[0], gain)
    next_rows, _, _ = apply_rms_norm(arrived, gain)

    dense_all = gathered(dense)
    prev_all = gathered(prev_rows)
    cot_all = gathered(cot)
    next_all = gathered(next_rows)

    mine = lax.dynamic_slice_in_dim(
        dense_all.reshape(-1, 2, owners, local), me, 1, axis=2
    )[:, :, 0].astype(F32)
    gate_next, gate_prev = mine[:, 0], mine[:, 1]

    gated, d_gate, d_up, products, weight_grads = [], [], [], [], []
    for j in range(local):
        pre_gate = dot(prev_all, wg[j], 1, 0)
        pre_up = dot(prev_all, wu[j], 1, 0)
        plain = dot(cot_all, wd[j], 1, 1)
        weight = gate_prev[:, j : j + 1]
        sigma = jax.nn.sigmoid(pre_gate)
        active = pre_gate * sigma
        hidden = active * pre_up
        products.append(jnp.sum(hidden * plain, axis=1))
        d_hidden = weight * plain
        gated.append((weight * hidden).astype(BF16))
        d_gate.append((d_hidden * pre_up * sigma * (1.0 + pre_gate * (1.0 - sigma))).astype(BF16))
        d_up.append((d_hidden * active).astype(BF16))
    row_grad = sum(dot(d_gate[j], wg[j], 1, 1) + dot(d_up[j], wu[j], 1, 1) for j in range(local))
    summed = lax.psum_scatter(row_grad.astype(BF16), "expert", scatter_dimension=0, tiled=True)
    products = jnp.stack(products, axis=1).astype(BF16).reshape(owners, tokens, local)
    products_back = lax.all_to_all(products, "expert", split_axis=0, concat_axis=0, tiled=True)

    mixed = 0.0
    for j in range(local):
        hidden = jax.nn.silu(dot(next_all, wg[j], 1, 0)) * dot(next_all, wu[j], 1, 0)
        mixed = mixed + dot((gate_next[:, j : j + 1] * hidden).astype(BF16), wd[j], 1, 0)
    mixed = lax.psum_scatter(mixed.astype(BF16), "expert", scatter_dimension=0, tiled=True)

    grad_gate = jnp.stack([dot(prev_all, d_gate[j], 0, 0).astype(BF16) for j in range(local)])
    grad_up = jnp.stack([dot(prev_all, d_up[j], 0, 0).astype(BF16) for j in range(local)])
    grad_down = jnp.stack([dot(gated[j], cot_all, 0, 0).astype(BF16) for j in range(local)])

    fwd_out = (arrived.astype(F32) + mixed.astype(F32)).astype(BF16)

    by_expert = jnp.transpose(products_back, (1, 0, 2)).reshape(tokens, experts_all).astype(F32)
    hit = routes_prev[0][:, :, None] == jnp.arange(experts_all, dtype=jnp.int32)
    gate_grad = jnp.sum(jnp.where(hit, by_expert[:, None, :], 0.0), axis=-1).astype(BF16)

    normalized_gradient = summed.astype(F32) * gain
    backward = cot.astype(F32) + scale * (
        normalized_gradient
        - unit_rows * jnp.mean(normalized_gradient * unit_rows, axis=-1, keepdims=True)
    )
    return (
        fwd_out[None],
        backward.astype(BF16)[None],
        gate_grad[None],
        grad_gate[None],
        grad_up[None],
        grad_down[None],
    )


def solution(mesh):
    tokens = P("section", "expert", None)
    weights = P("section", "expert", None, None)
    return jax.shard_map(
        per_device,
        mesh=mesh,
        in_specs=(tokens, tokens, tokens, P("section", None), weights, weights, weights)
        + (tokens,) * 4,
        out_specs=(tokens, tokens, tokens, weights, weights, weights),
        check_vma=False,
    )
```

```python
import functools

import jax
import jax.numpy as jnp
from jax import lax
from jax.experimental import pallas as pl
from jax.experimental.pallas import tpu as pltpu
from jax.sharding import PartitionSpec as P

EPS = 1e-06
F32 = jnp.float32
BF16 = jnp.bfloat16
LANES = 128
VMEM = pl.BlockSpec(memory_space=pltpu.VMEM)


class Ring:
    def __init__(self, sections, owners):
        bits = owners.bit_length() - 1
        self.n = owners
        self.half = owners // 2
        self.nz = 1 << ((bits + 1) // 2)
        self.ny = owners // self.nz
        self.section = lax.axis_index("section")
        self.sections = sections
        self.me = lax.axis_index("expert")
        z, y = self.me // self.ny, self.me % self.ny
        self.place = y * self.nz + z + (y % 2) * (self.nz - 1 - 2 * z)
        self.sides = (self.owner(1), self.owner(-1))

    def owner(self, offset):
        p = (self.place + offset + self.n) % self.n
        y, r = p // self.nz, p % self.nz
        return (r + (y % 2) * (self.nz - 1 - 2 * r)) * self.ny + y

    def peer(self, offset):
        return (self.me + offset) % self.n

    def device(self, expert):
        return (self.section, expert)

    def shifted(self, by):
        return ((self.section + by + self.sections) % self.sections, self.me)

    def greet(self, sections_too):
        barrier = pltpu.get_barrier_semaphore()
        targets = [self.device(self.peer(r)) for r in range(1, self.n)]
        if sections_too:
            targets += [self.shifted(1), self.shifted(-1)]
        for target in targets:
            pl.semaphore_signal(
                barrier, inc=1, device_id=target, device_id_type=pl.DeviceIdType.MESH
            )
        pl.semaphore_wait(barrier, len(targets))


def send(src, dst, send_sem, recv_sem, device):
    return pltpu.make_async_remote_copy(
        src_ref=src,
        dst_ref=dst,
        send_sem=send_sem,
        recv_sem=recv_sem,
        device_id=device,
        device_id_type=pl.DeviceIdType.MESH,
    )


def normed(rows, gain):
    values = rows.astype(F32)
    scale = lax.rsqrt(jnp.mean(values * values, axis=-1, keepdims=True) + EPS)
    return (values * scale * gain).astype(BF16)


def gather_kernel(
    sections, owners,
    act_ref, stash_ref, cot_ref, gain_ref, dense_ref,
    arrived_ref, next_ref, prev_ref, cots_ref, gates_ref,
    shift_send, shift_recv, gate_send, gate_recv, ring_send, ring_recv,
):
    ring = Ring(sections, owners)
    me, half = ring.me, ring.half
    width = stash_ref.shape[1]
    cut = width // 2
    ring.greet(True)
    cot_shift = send(cot_ref, cots_ref.at[me], shift_send.at[0], shift_recv.at[0], ring.shifted(-1))
    act_shift = send(act_ref, arrived_ref, shift_send.at[1], shift_recv.at[1], ring.shifted(1))
    cot_shift.start()
    act_shift.start()
    prev_ref[me] = normed(stash_ref[...], gain_ref[...])
    gates_ref[me] = dense_ref[...]
    buffers = (prev_ref, cots_ref, next_ref)

    def hops(t, k):
        made = []
        for d, way in enumerate((1, -1)):
            block = ring.owner(-way * k)
            ref = buffers[t].at[block]
            if k == half - 1:
                ref = ref.at[:, pl.ds(d * cut, cut)]
            made.append(
                send(ref, ref, ring_send.at[t, d, k], ring_recv.at[t, d, k], ring.device(ring.sides[d]))
            )
        return made

    flying = {}

    def start(t, k):
        flying[t, k] = hops(t, k)
        for copy in flying[t, k]:
            copy.start()

    start(0, 0)
    gate_copies = [
        send(dense_ref, gates_ref.at[me], gate_send.at[r - 1], gate_recv.at[r - 1], ring.device(ring.peer(r)))
        for r in range(1, owners)
    ]
    for copy in gate_copies:
        copy.start()
    cot_shift.wait()
    start(1, 0)
    act_shift.wait()
    next_ref[me] = normed(arrived_ref[...], gain_ref[...])
    start(2, 0)
    for k in range(1, half):
        for t in range(3):
            for copy in flying[t, k - 1]:
                copy.wait_recv()
            start(t, k)
    for t in range(3):
        for copy in flying[t, half - 1]:
            copy.wait_recv()
        for k in range(half):
            for copy in flying[t, k]:
                copy.wait_send()
    for copy in gate_copies:
        copy.wait()


def gather_call(sections, owners, act, stash, cot, gain, dense):
    tokens, width = stash.shape
    half = owners // 2
    every = jax.ShapeDtypeStruct((owners, tokens, width), BF16)
    return pl.pallas_call(
        functools.partial(gather_kernel, sections, owners),
        out_shape=(
            jax.ShapeDtypeStruct((tokens, width), BF16),
            every, every, every,
            jax.ShapeDtypeStruct((owners,) + dense.shape, BF16),
        ),
        in_specs=[VMEM] * 5,
        out_specs=(VMEM,) * 5,
        scratch_shapes=[
            pltpu.SemaphoreType.DMA((2,)),
            pltpu.SemaphoreType.DMA((2,)),
            pltpu.SemaphoreType.DMA((owners - 1,)),
            pltpu.SemaphoreType.DMA((owners - 1,)),
            pltpu.SemaphoreType.DMA((3, 2, half)),
            pltpu.SemaphoreType.DMA((3, 2, half)),
        ],
        compiler_params=pltpu.CompilerParams(collective_id=0, has_side_effects=True),
    )(act, stash, cot, gain, dense)


def reduce_kernel(
    sections, owners, count, *refs,
):
    parts, products_ref = refs[:count], refs[count]
    totals, returned_ref = refs[count + 1 : 2 * count + 1], refs[2 * count + 1]
    outgoing, arriving, small_send, small_recv, ring_send, ring_recv = refs[2 * count + 2 :]
    ring = Ring(sections, owners)
    me, half = ring.me, ring.half
    width = parts[0].shape[2]
    cut = width // 2
    ring.greet(False)

    def start(t, k):
        made = []
        for d, way in enumerate((1, -1)):
            block = ring.owner(way * (half - k))
            cols = pl.ds(d * cut, cut)
            if k == 0:
                src = parts[t].at[block, :, cols]
                dst = arriving.at[t, d, k, :, cols]
            else:
                src, dst = outgoing.at[t, d, k - 1], arriving.at[t, d, k]
                if k == 1:
                    rest = pl.ds((1 - d) * cut, cut)
                    src[:, rest] = parts[t][block, :, rest]
                    src[:, cols] = (
                        parts[t][block, :, cols].astype(F32)
                        + arriving[t, d, k - 1, :, cols].astype(F32)
                    ).astype(BF16)
                else:
                    src[...] = (
                        parts[t][block].astype(F32) + arriving[t, d, k - 1].astype(F32)
                    ).astype(BF16)
            made.append(
                send(src, dst, ring_send.at[t, d, k], ring_recv.at[t, d, k], ring.device(ring.sides[d]))
            )
            made[-1].start()
        flying[t, k] = made

    flying = {}
    for t in range(count):
        start(t, 0)
    small = [
        send(
            products_ref.at[ring.peer(r)], returned_ref.at[me],
            small_send.at[r - 1], small_recv.at[r - 1], ring.device(ring.peer(r)),
        )
        for r in range(1, owners)
    ]
    for copy in small:
        copy.start()
    returned_ref[me] = products_ref[me]
    for k in range(1, half):
        for t in range(count):
            for copy in flying[t, k - 1]:
                copy.wait_recv()
            start(t, k)
    for t in range(count):
        for copy in flying[t, half - 1]:
            copy.wait_recv()
        totals[t][...] = (
            parts[t][me].astype(F32)
            + arriving[t, 0, half - 1].astype(F32)
            + arriving[t, 1, half - 1].astype(F32)
        )
    for t in range(count):
        for k in range(half):
            for copy in flying[t, k]:
                copy.wait_send()
    for copy in small:
        copy.wait()


def reduce_call(sections, owners, products, *parts):
    count = len(parts)
    _, tokens, width = parts[0].shape
    half = owners // 2
    return pl.pallas_call(
        functools.partial(reduce_kernel, sections, owners, count),
        out_shape=(jax.ShapeDtypeStruct((tokens, width), F32),) * count
        + (jax.ShapeDtypeStruct(products.shape, BF16),),
        in_specs=[VMEM] * (count + 1),
        out_specs=(VMEM,) * (count + 1),
        scratch_shapes=[
            pltpu.VMEM((count, 2, half - 1, tokens, width), BF16),
            pltpu.VMEM((count, 2, half, tokens, width), BF16),
            pltpu.SemaphoreType.DMA((owners - 1,)),
            pltpu.SemaphoreType.DMA((owners - 1,)),
            pltpu.SemaphoreType.DMA((count, 2, half)),
            pltpu.SemaphoreType.DMA((count, 2, half)),
        ],
        compiler_params=pltpu.CompilerParams(collective_id=1, has_side_effects=True),
    )(*parts, products)


def apply_rms_norm(rows, gain):
    values = rows.astype(F32)
    scale = lax.rsqrt(jnp.mean(values * values, axis=-1, keepdims=True) + EPS)
    unit = values * scale
    return (unit * gain).astype(BF16), unit, scale


def dense_gates(routes, gates, experts_all):
    hit = routes[:, :, None] == jnp.arange(experts_all, dtype=jnp.int32)
    return jnp.sum(jnp.where(hit, gates.astype(F32)[:, :, None], 0.0), axis=1).astype(BF16)


def dot(a, b, ca, cb):
    return lax.dot_general(a, b, (((ca,), (cb,)), ((), ())), preferred_element_type=F32)


def per_device(
    sent_acts,
    stash,
    cotangents,
    norm_gain,
    w_gate,
    w_up,
    w_down,
    routes_next,
    gates_next,
    routes_prev,
    gates_prev,
):
    owners = lax.axis_size("expert")
    me = lax.axis_index("expert")
    gain = norm_gain[0].astype(F32)
    wg, wu, wd = w_gate[0], w_up[0], w_down[0]
    local, width, hidden_units = wg.shape
    experts_all = local * owners
    tokens = stash.shape[1]

    dense = jnp.concatenate(
        [
            dense_gates(routes_next[0], gates_next[0], experts_all),
            dense_gates(routes_prev[0], gates_prev[0], experts_all),
        ],
        axis=1,
    )
    dense = jnp.pad(dense, ((0, 0), (0, LANES - dense.shape[1])))
    sections = lax.axis_size("section")
    _, unit_rows, scale = apply_rms_norm(stash[0], gain)
    arrived, next_all, prev_all, cot_all, dense_all = gather_call(
        sections, owners, sent_acts[0], stash[0], cotangents[0], gain[None], dense
    )
    cot = lax.dynamic_index_in_dim(cot_all, me, 0, keepdims=False)
    next_all, prev_all, cot_all = (a.reshape(-1, width) for a in (next_all, prev_all, cot_all))
    dense_all = dense_all.reshape(-1, LANES)[:, : 2 * experts_all]

    mine = lax.dynamic_slice_in_dim(
        dense_all.reshape(-1, 2, owners, local), me, 1, axis=2
    )[:, :, 0].astype(F32)
    gate_next, gate_prev = mine[:, 0], mine[:, 1]

    gated, d_gate, d_up, products, weight_grads = [], [], [], [], []
    for j in range(local):
        pre_gate = dot(prev_all, wg[j], 1, 0)
        pre_up = dot(prev_all, wu[j], 1, 0)
        plain = dot(cot_all, wd[j], 1, 1)
        weight = gate_prev[:, j : j + 1]
        sigma = jax.nn.sigmoid(pre_gate)
        active = pre_gate * sigma
        hidden = active * pre_up
        products.append(jnp.sum(hidden * plain, axis=1))
        d_hidden = weight * plain
        gated.append((weight * hidden).astype(BF16))
        d_gate.append((d_hidden * pre_up * sigma * (1.0 + pre_gate * (1.0 - sigma))).astype(BF16))
        d_up.append((d_hidden * active).astype(BF16))
    row_grad = sum(dot(d_gate[j], wg[j], 1, 1) + dot(d_up[j], wu[j], 1, 1) for j in range(local))
    products = jnp.stack(products, axis=1).astype(BF16).reshape(owners, tokens, local)
    products = jnp.pad(products, ((0, 0), (0, 0), (0, LANES - local)))

    mixed = 0.0
    for j in range(local):
        hidden = jax.nn.silu(dot(next_all, wg[j], 1, 0)) * dot(next_all, wu[j], 1, 0)
        mixed = mixed + dot((gate_next[:, j : j + 1] * hidden).astype(BF16), wd[j], 1, 0)
    summed, mixed, products_back = reduce_call(
        sections,
        owners,
        products,
        row_grad.astype(BF16).reshape(owners, tokens, width),
        mixed.astype(BF16).reshape(owners, tokens, width),
    )
    products_back = products_back[:, :, :local]

    grad_gate = jnp.stack([dot(prev_all, d_gate[j], 0, 0).astype(BF16) for j in range(local)])
    grad_up = jnp.stack([dot(prev_all, d_up[j], 0, 0).astype(BF16) for j in range(local)])
    grad_down = jnp.stack([dot(gated[j], cot_all, 0, 0).astype(BF16) for j in range(local)])

    fwd_out = (arrived.astype(F32) + mixed).astype(BF16)

    by_expert = jnp.transpose(products_back, (1, 0, 2)).reshape(tokens, experts_all).astype(F32)
    hit = routes_prev[0][:, :, None] == jnp.arange(experts_all, dtype=jnp.int32)
    gate_grad = jnp.sum(jnp.where(hit, by_expert[:, None, :], 0.0), axis=-1).astype(BF16)

    normalized_gradient = summed * gain
    backward = cot.astype(F32) + scale * (
        normalized_gradient
        - unit_rows * jnp.mean(normalized_gradient * unit_rows, axis=-1, keepdims=True)
    )
    return (
        fwd_out[None],
        backward.astype(BF16)[None],
        gate_grad[None],
        grad_gate[None],
        grad_up[None],
        grad_down[None],
    )


def solution(mesh):
    tokens = P("section", "expert", None)
    weights = P("section", "expert", None, None)
    return jax.shard_map(
        per_device,
        mesh=mesh,
        in_specs=(tokens, tokens, tokens, P("section", None), weights, weights, weights)
        + (tokens,) * 4,
        out_specs=(tokens, tokens, tokens, weights, weights, weights),
        check_vma=False,
    )
```

```python
import functools

import jax
import jax.numpy as jnp
from jax import lax
from jax.experimental import pallas as pl
from jax.experimental.pallas import tpu as pltpu
from jax.sharding import PartitionSpec as P

EPS = 1e-06
F32 = jnp.float32
BF16 = jnp.bfloat16
LANES = 128
VMEM = pl.BlockSpec(memory_space=pltpu.VMEM)


class Ring:
    def __init__(self, sections, owners):
        bits = owners.bit_length() - 1
        self.n = owners
        self.half = owners // 2
        self.nz = 1 << ((bits + 1) // 2)
        self.ny = owners // self.nz
        self.section = lax.axis_index("section")
        self.sections = sections
        self.me = lax.axis_index("expert")
        z, y = self.me // self.ny, self.me % self.ny
        self.place = y * self.nz + z + (y % 2) * (self.nz - 1 - 2 * z)
        self.sides = (self.owner(1), self.owner(-1))

    def owner(self, offset):
        p = (self.place + offset + self.n) % self.n
        y, r = p // self.nz, p % self.nz
        return (r + (y % 2) * (self.nz - 1 - 2 * r)) * self.ny + y

    def peer(self, offset):
        return (self.me + offset) % self.n

    def device(self, expert):
        return (self.section, expert)

    def shifted(self, by):
        return ((self.section + by + self.sections) % self.sections, self.me)

    def greet(self, sections_too):
        barrier = pltpu.get_barrier_semaphore()
        targets = [self.device(self.peer(r)) for r in range(1, self.n)]
        if sections_too:
            targets += [self.shifted(1), self.shifted(-1)]
        for target in targets:
            pl.semaphore_signal(
                barrier, inc=1, device_id=target, device_id_type=pl.DeviceIdType.MESH
            )
        pl.semaphore_wait(barrier, len(targets))


def send(src, dst, send_sem, recv_sem, device):
    return pltpu.make_async_remote_copy(
        src_ref=src,
        dst_ref=dst,
        send_sem=send_sem,
        recv_sem=recv_sem,
        device_id=device,
        device_id_type=pl.DeviceIdType.MESH,
    )


def normed(rows, gain):
    values = rows.astype(F32)
    scale = lax.rsqrt(jnp.mean(values * values, axis=-1, keepdims=True) + EPS)
    return (values * scale * gain).astype(BF16)


def dot(a, b, ca, cb):
    return lax.dot_general(a, b, (((ca,), (cb,)), ((), ())), preferred_element_type=F32)


def flat(ref):
    value = ref[...]
    return value.reshape(-1, value.shape[-1])


def tile_of(size):
    return 256 if size % 256 == 0 else LANES


def columns(i, tile):
    return pl.ds(pl.multiple_of(i * tile, tile), tile)


def gate_column(gates_ref, index):
    rows = flat(gates_ref).astype(F32)
    lane = lax.broadcasted_iota(jnp.int32, rows.shape, 1)
    return jnp.sum(jnp.where(lane == index, rows, 0.0), axis=1, keepdims=True)


def load_weights(hbm, held, sems):
    copies = [pltpu.make_async_copy(h, v, sems.at[i]) for i, (h, v) in enumerate(zip(hbm, held))]
    for copy in copies:
        copy.start()
    return copies


def gather_kernel(
    sections, owners,
    act_ref, stash_ref, cot_ref, gain_ref, dense_ref, wg_hbm, wu_hbm, wd_hbm,
    arrived_ref, next_ref, prev_ref, cots_ref, gates_ref,
    d_gate_ref, d_up_ref, gated_ref, row_ref, products_ref,
    wg, wu, wd, pre_gate, pre_up, sums,
    shift_send, shift_recv, gate_send, gate_recv, ring_send, ring_recv, weight_sem,
):
    ring = Ring(sections, owners)
    me, half = ring.me, ring.half
    tokens, width = stash_ref.shape
    local, _, units = wg.shape
    cut = width // 2
    loads = load_weights((wg_hbm, wu_hbm, wd_hbm), (wg, wu, wd), weight_sem)
    ring.greet(True)
    cot_shift = send(cot_ref, cots_ref.at[me], shift_send.at[0], shift_recv.at[0], ring.shifted(-1))
    act_shift = send(act_ref, arrived_ref, shift_send.at[1], shift_recv.at[1], ring.shifted(1))
    cot_shift.start()
    act_shift.start()
    prev_ref[me] = normed(stash_ref[...], gain_ref[...])
    gates_ref[me] = dense_ref[...]
    buffers = (prev_ref, cots_ref, next_ref)
    flying = {}

    def start(t, k):
        made = []
        for d, way in enumerate((1, -1)):
            block = ring.owner(-way * k)
            ref = buffers[t].at[block]
            if k == half - 1:
                ref = ref.at[:, pl.ds(d * cut, cut)]
            made.append(
                send(ref, ref, ring_send.at[t, d, k], ring_recv.at[t, d, k], ring.device(ring.sides[d]))
            )
        flying[t, k] = made
        for copy in made:
            copy.start()

    def arrive(t, k):
        for copy in flying[t, k]:
            copy.wait_recv()

    def advance(t, k):
        if k < half:
            arrive(t, k - 1)
            start(t, k)

    tile = tile_of(units)

    def pre_activations(j):
        @pl.loop(0, units // tile)
        def _(i):
            cols = columns(i, tile)
            rows = flat(prev_ref)
            pre_gate[j, :, cols] = dot(rows, wg[j, :, cols], 1, 0)
            pre_up[j, :, cols] = dot(rows, wu[j, :, cols], 1, 0)

    def gradients(j):
        weight = gate_column(gates_ref, (owners + me) * local + j)
        sums[j] = jnp.zeros(sums.shape[1:], F32)

        @pl.loop(0, units // tile)
        def _(i):
            cols = columns(i, tile)
            plain = dot(flat(cots_ref), wd[j, cols, :], 1, 1)
            gate, up = pre_gate[j, :, cols], pre_up[j, :, cols]
            sigma = jax.nn.sigmoid(gate)
            active = gate * sigma
            hidden = active * up
            d_hidden = weight * plain
            sums[j] += jnp.sum(hidden * plain, axis=1, keepdims=True)
            gated_ref[j, :, cols] = (weight * hidden).astype(BF16)
            d_gate_ref[j, :, cols] = (d_hidden * up * sigma * (1.0 + gate * (1.0 - sigma))).astype(BF16)
            d_up_ref[j, :, cols] = (d_hidden * active).astype(BF16)

    wide = tile_of(width)

    def row_gradients(low, high):
        @pl.loop(low, high)
        def _(i):
            cols = columns(i, wide)
            total = 0.0
            for j in range(local):
                total = total + dot(d_gate_ref[j], wg[j, cols, :], 1, 1)
                total = total + dot(d_up_ref[j], wu[j, cols, :], 1, 1)
            row_ref[:, :, cols] = total.astype(BF16).reshape(owners, tokens, wide)

    start(0, 0)
    gate_copies = [
        send(dense_ref, gates_ref.at[me], gate_send.at[r - 1], gate_recv.at[r - 1], ring.device(ring.peer(r)))
        for r in range(1, owners)
    ]
    for copy in gate_copies:
        copy.start()
    cot_shift.wait()
    start(1, 0)
    act_shift.wait()
    next_ref[me] = normed(arrived_ref[...], gain_ref[...])
    for k in range(1, half):
        advance(0, k)
        if k >= 2:
            advance(1, k - 1)
    for copy in loads:
        copy.wait()
    for copy in gate_copies:
        copy.wait()
    arrive(0, half - 1)
    start(2, 0)
    pre_activations(0)
    advance(1, half - 1)
    for j in range(1, local):
        pre_activations(j)
    advance(2, 1)
    arrive(1, half - 1)
    for j in range(local):
        gradients(j)
        advance(2, 2 + j)
    steps = list(range(2 + local, half))
    row_gradients(0, width // wide // 2)
    for k in steps:
        advance(2, k)
    row_gradients(width // wide // 2, width // wide)
    lane = lax.broadcasted_iota(jnp.int32, sums.shape[1:], 1)
    total = jnp.zeros(sums.shape[1:], F32)
    for j in range(local):
        total = jnp.where(lane == j, sums[j], total)
    products_ref[...] = total.astype(BF16).reshape(products_ref.shape)
    arrive(2, half - 1)
    for t in range(3):
        for k in range(half):
            for copy in flying[t, k]:
                copy.wait_send()


ANY = pl.BlockSpec(memory_space=pl.ANY)
VMEM_LIMIT = 60 * 2**20


def gather_call(sections, owners, act, stash, cot, gain, dense, wg, wu, wd):
    tokens, width = stash.shape
    local, _, units = wg.shape
    half = owners // 2
    every = jax.ShapeDtypeStruct((owners, tokens, width), BF16)
    inner = jax.ShapeDtypeStruct((local, owners * tokens, units), BF16)
    small = jax.ShapeDtypeStruct((owners,) + dense.shape, BF16)
    return pl.pallas_call(
        functools.partial(gather_kernel, sections, owners),
        out_shape=(
            jax.ShapeDtypeStruct((tokens, width), BF16),
            every, every, every, small, inner, inner, inner, every, small,
        ),
        in_specs=[VMEM] * 5 + [ANY] * 3,
        out_specs=(VMEM,) * 10,
        scratch_shapes=[
            pltpu.VMEM(wg.shape, BF16),
            pltpu.VMEM(wu.shape, BF16),
            pltpu.VMEM(wd.shape, BF16),
            pltpu.VMEM(inner.shape, F32),
            pltpu.VMEM(inner.shape, F32),
            pltpu.VMEM((local, owners * tokens, LANES), F32),
            pltpu.SemaphoreType.DMA((2,)),
            pltpu.SemaphoreType.DMA((2,)),
            pltpu.SemaphoreType.DMA((owners - 1,)),
            pltpu.SemaphoreType.DMA((owners - 1,)),
            pltpu.SemaphoreType.DMA((3, 2, half)),
            pltpu.SemaphoreType.DMA((3, 2, half)),
            pltpu.SemaphoreType.DMA((3,)),
        ],
        compiler_params=pltpu.CompilerParams(
            collective_id=0, has_side_effects=True, vmem_limit_bytes=VMEM_LIMIT
        ),
    )(act, stash, cot, gain, dense, wg, wu, wd)


def reduce_kernel(
    sections, owners,
    row_ref, products_ref, next_ref, prev_ref, cots_ref, gates_ref,
    d_gate_ref, d_up_ref, gated_ref, wg_hbm, wu_hbm, wd_hbm,
    summed_ref, mixed_ref, returned_ref, grad_gate_hbm, grad_up_hbm, grad_down_hbm,
    wg, wu, wd, hidden_ref, part_ref,
    outgoing, arriving, small_send, small_recv, ring_send, ring_recv, weight_sem, grad_sem,
):
    parts, totals, count = (row_ref, part_ref), (summed_ref, mixed_ref), 2
    local, _, units = wg.shape
    loads = load_weights((wg_hbm, wu_hbm, wd_hbm), (wg, wu, wd), weight_sem)
    ring = Ring(sections, owners)
    me, half = ring.me, ring.half
    width = parts[0].shape[2]
    cut = width // 2
    ring.greet(False)

    def start(t, k):
        made = []
        for d, way in enumerate((1, -1)):
            block = ring.owner(way * (half - k))
            cols = pl.ds(d * cut, cut)
            if k == 0:
                src = parts[t].at[block, :, cols]
                dst = arriving.at[t, d, k, :, cols]
            else:
                src, dst = outgoing.at[t, d, k - 1], arriving.at[t, d, k]
                if k == 1:
                    rest = pl.ds((1 - d) * cut, cut)
                    src[:, rest] = parts[t][block, :, rest]
                    src[:, cols] = (
                        parts[t][block, :, cols].astype(F32)
                        + arriving[t, d, k - 1, :, cols].astype(F32)
                    ).astype(BF16)
                else:
                    src[...] = (
                        parts[t][block].astype(F32) + arriving[t, d, k - 1].astype(F32)
                    ).astype(BF16)
            made.append(
                send(src, dst, ring_send.at[t, d, k], ring_recv.at[t, d, k], ring.device(ring.sides[d]))
            )
            made[-1].start()
        flying[t, k] = made

    flying = {}
    start(0, 0)
    small = [
        send(
            products_ref.at[ring.peer(r)], returned_ref.at[me],
            small_send.at[r - 1], small_recv.at[r - 1], ring.device(ring.peer(r)),
        )
        for r in range(1, owners)
    ]
    for copy in small:
        copy.start()
    returned_ref[me] = products_ref[me]
    def advance(t, k):
        if k < half:
            for copy in flying[t, k - 1]:
                copy.wait_recv()
            start(t, k)

    def finish(t):
        for copy in flying[t, half - 1]:
            copy.wait_recv()
        totals[t][...] = (
            parts[t][me].astype(F32)
            + arriving[t, 0, half - 1].astype(F32)
            + arriving[t, 1, half - 1].astype(F32)
        )

    tile, wide = tile_of(units), tile_of(width)

    def hidden(j):
        weight = gate_column(gates_ref, me * local + j)

        @pl.loop(0, units // tile)
        def _(i):
            cols = columns(i, tile)
            rows = flat(next_ref)
            gate = dot(rows, wg[j, :, cols], 1, 0)
            up = dot(rows, wu[j, :, cols], 1, 0)
            hidden_ref[j, :, cols] = (weight * (gate * jax.nn.sigmoid(gate) * up)).astype(BF16)

    def mix(low, high):
        @pl.loop(low, high)
        def _(i):
            cols = columns(i, wide)
            total = 0.0
            for j in range(local):
                total = total + dot(hidden_ref[j], wd[j, :, cols], 1, 0)
            part_ref[:, :, cols] = total.astype(BF16).reshape(part_ref.shape[:2] + (wide,))

    grads = []

    def weight_gradient(held, out_hbm, index, j):
        rows_size = held.shape[1]
        step = tile_of(rows_size)

        @pl.loop(0, rows_size // step)
        def _(i):
            rows = columns(i, step)
            if index == 2:
                left, right = gated_ref[j, :, rows], flat(cots_ref)
            else:
                left = prev_ref[:, :, rows].reshape(-1, step)
                right = (d_gate_ref, d_up_ref)[index][j]
            held[j, rows, :] = dot(left, right, 0, 0).astype(BF16)

        copy = pltpu.make_async_copy(held.at[j], out_hbm.at[j], grad_sem.at[index, j])
        copy.start()
        grads.append(copy)

    for copy in loads:
        copy.wait()
    for j in range(local):
        hidden(j)
        advance(0, 1 + j)
    mix(0, width // wide // 2)
    for k in range(1 + local, half):
        advance(0, k)
    mix(width // wide // 2, width // wide)
    start(1, 0)
    finish(0)
    k = 1
    for index, (held, out) in enumerate(((wg, grad_gate_hbm), (wu, grad_up_hbm), (wd, grad_down_hbm))):
        for j in range(local):
            weight_gradient(held, out, index, j)
            advance(1, k)
            k += 1
    for k in range(k, half):
        advance(1, k)
    finish(1)
    for copy in grads:
        copy.wait()
    for t in range(count):
        for k in range(half):
            for copy in flying[t, k]:
                copy.wait_send()
    for copy in small:
        copy.wait()


def reduce_call(sections, owners, row, products, rows_next, prev, cots, gates, inner, weights):
    _, tokens, width = row.shape
    half = owners // 2
    total = jax.ShapeDtypeStruct((tokens, width), F32)
    return pl.pallas_call(
        functools.partial(reduce_kernel, sections, owners),
        out_shape=(total, total, jax.ShapeDtypeStruct(products.shape, BF16))
        + tuple(jax.ShapeDtypeStruct(w.shape, BF16) for w in weights),
        in_specs=[VMEM] * 9 + [ANY] * 3,
        out_specs=(VMEM,) * 3 + (ANY,) * 3,
        scratch_shapes=[pltpu.VMEM(w.shape, BF16) for w in weights]
        + [
            pltpu.VMEM(inner[0].shape, BF16),
            pltpu.VMEM(row.shape, BF16),
            pltpu.VMEM((2, 2, half - 1, tokens, width), BF16),
            pltpu.VMEM((2, 2, half, tokens, width), BF16),
            pltpu.SemaphoreType.DMA((owners - 1,)),
            pltpu.SemaphoreType.DMA((owners - 1,)),
            pltpu.SemaphoreType.DMA((2, 2, half)),
            pltpu.SemaphoreType.DMA((2, 2, half)),
            pltpu.SemaphoreType.DMA((3,)),
            pltpu.SemaphoreType.DMA((3, weights[0].shape[0])),
        ],
        compiler_params=pltpu.CompilerParams(
            collective_id=1, has_side_effects=True, vmem_limit_bytes=VMEM_LIMIT
        ),
    )(row, products, rows_next, prev, cots, gates, *inner, *weights)


def apply_rms_norm(rows, gain):
    values = rows.astype(F32)
    scale = lax.rsqrt(jnp.mean(values * values, axis=-1, keepdims=True) + EPS)
    unit = values * scale
    return (unit * gain).astype(BF16), unit, scale


def dense_gates(routes, gates, experts_all):
    hit = routes[:, :, None] == jnp.arange(experts_all, dtype=jnp.int32)
    return jnp.sum(jnp.where(hit, gates.astype(F32)[:, :, None], 0.0), axis=1).astype(BF16)


def per_device(
    sent_acts,
    stash,
    cotangents,
    norm_gain,
    w_gate,
    w_up,
    w_down,
    routes_next,
    gates_next,
    routes_prev,
    gates_prev,
):
    owners = lax.axis_size("expert")
    me = lax.axis_index("expert")
    gain = norm_gain[0].astype(F32)
    wg, wu, wd = w_gate[0], w_up[0], w_down[0]
    local, width, hidden_units = wg.shape
    experts_all = local * owners
    tokens = stash.shape[1]

    dense = jnp.concatenate(
        [
            dense_gates(routes_next[0], gates_next[0], experts_all),
            dense_gates(routes_prev[0], gates_prev[0], experts_all),
        ],
        axis=1,
    )
    dense = jnp.pad(dense, ((0, 0), (0, LANES - dense.shape[1])))
    sections = lax.axis_size("section")
    _, unit_rows, scale = apply_rms_norm(stash[0], gain)
    weights = (wg, wu, wd)
    arrived, next_all, prev_all, cot_all, dense_all, d_gate, d_up, gated, row, products = gather_call(
        sections, owners, sent_acts[0], stash[0], cotangents[0], gain[None], dense, *weights
    )
    cot = lax.dynamic_index_in_dim(cot_all, me, 0, keepdims=False)
    summed, mixed, products_back, grad_gate, grad_up, grad_down = reduce_call(
        sections, owners, row, products, next_all, prev_all, cot_all, dense_all,
        (d_gate, d_up, gated), weights,
    )
    products_back = products_back[:, :, :local]

    fwd_out = (arrived.astype(F32) + mixed).astype(BF16)

    by_expert = jnp.transpose(products_back, (1, 0, 2)).reshape(tokens, experts_all).astype(F32)
    hit = routes_prev[0][:, :, None] == jnp.arange(experts_all, dtype=jnp.int32)
    gate_grad = jnp.sum(jnp.where(hit, by_expert[:, None, :], 0.0), axis=-1).astype(BF16)

    normalized_gradient = summed * gain
    backward = cot.astype(F32) + scale * (
        normalized_gradient
        - unit_rows * jnp.mean(normalized_gradient * unit_rows, axis=-1, keepdims=True)
    )
    return (
        fwd_out[None],
        backward.astype(BF16)[None],
        gate_grad[None],
        grad_gate[None],
        grad_up[None],
        grad_down[None],
    )


def solution(mesh):
    tokens = P("section", "expert", None)
    weights = P("section", "expert", None, None)
    return jax.shard_map(
        per_device,
        mesh=mesh,
        in_specs=(tokens, tokens, tokens, P("section", None), weights, weights, weights)
        + (tokens,) * 4,
        out_specs=(tokens, tokens, tokens, weights, weights, weights),
        check_vma=False,
    )
```

```python
import functools

import jax
import jax.numpy as jnp
from jax import lax
from jax.experimental import pallas as pl
from jax.experimental.pallas import tpu as pltpu
from jax.sharding import PartitionSpec as P

EPS = 1e-06
F32 = jnp.float32
BF16 = jnp.bfloat16
LANES = 128
VMEM = pl.BlockSpec(memory_space=pltpu.VMEM)


class Ring:
    def __init__(self, sections, owners):
        bits = owners.bit_length() - 1
        self.n = owners
        self.half = owners // 2
        self.nz = 1 << ((bits + 1) // 2)
        self.ny = owners // self.nz
        self.section = lax.axis_index("section")
        self.sections = sections
        self.me = lax.axis_index("expert")
        z, y = self.me // self.ny, self.me % self.ny
        self.place = y * self.nz + z + (y % 2) * (self.nz - 1 - 2 * z)
        self.sides = (self.owner(1), self.owner(-1))

    def owner(self, offset):
        p = (self.place + offset + self.n) % self.n
        y, r = p // self.nz, p % self.nz
        return (r + (y % 2) * (self.nz - 1 - 2 * r)) * self.ny + y

    def peer(self, offset):
        return (self.me + offset) % self.n

    def device(self, expert):
        return (self.section, expert)

    def shifted(self, by):
        return ((self.section + by + self.sections) % self.sections, self.me)

    def greet(self, sections_too):
        barrier = pltpu.get_barrier_semaphore()
        targets = [self.device(self.peer(r)) for r in range(1, self.n)]
        if sections_too:
            targets += [self.shifted(1), self.shifted(-1)]
        for target in targets:
            pl.semaphore_signal(
                barrier, inc=1, device_id=target, device_id_type=pl.DeviceIdType.MESH
            )
        pl.semaphore_wait(barrier, len(targets))


def send(src, dst, send_sem, recv_sem, device):
    return pltpu.make_async_remote_copy(
        src_ref=src,
        dst_ref=dst,
        send_sem=send_sem,
        recv_sem=recv_sem,
        device_id=device,
        device_id_type=pl.DeviceIdType.MESH,
    )


def normed(rows, gain):
    values = rows.astype(F32)
    scale = lax.rsqrt(jnp.mean(values * values, axis=-1, keepdims=True) + EPS)
    return (values * scale * gain).astype(BF16)


def dot(a, b, ca, cb):
    return lax.dot_general(a, b, (((ca,), (cb,)), ((), ())), preferred_element_type=F32)


def flat(ref):
    value = ref[...]
    return value.reshape(-1, value.shape[-1])


def tile_of(size):
    return 256 if size % 256 == 0 else LANES


def columns(i, tile):
    return pl.ds(pl.multiple_of(i * tile, tile), tile)


def gate_column(gates_ref, index):
    rows = flat(gates_ref).astype(F32)
    lane = lax.broadcasted_iota(jnp.int32, rows.shape, 1)
    return jnp.sum(jnp.where(lane == index, rows, 0.0), axis=1, keepdims=True)


def load_weights(hbm, held, sems):
    copies = [pltpu.make_async_copy(h, v, sems.at[i]) for i, (h, v) in enumerate(zip(hbm, held))]
    for copy in copies:
        copy.start()
    return copies


def gather_kernel(
    sections, owners,
    act_ref, stash_ref, cot_ref, gain_ref, dense_ref, wg_hbm, wu_hbm, wd_hbm,
    arrived_ref, next_ref, prev_ref, cots_ref, gates_ref,
    d_gate_ref, d_up_ref, gated_ref, row_ref, products_ref,
    wg, wu, wd, pre_gate, pre_up, sums,
    shift_send, shift_recv, gate_send, gate_recv, ring_send, ring_recv, weight_sem,
):
    ring = Ring(sections, owners)
    me, half = ring.me, ring.half
    tokens, width = stash_ref.shape
    local, _, units = wg.shape
    cut = width // 2
    loads = load_weights((wg_hbm, wu_hbm, wd_hbm), (wg, wu, wd), weight_sem)
    ring.greet(True)
    cot_shift = send(cot_ref, cots_ref.at[me], shift_send.at[0], shift_recv.at[0], ring.shifted(-1))
    act_shift = send(act_ref, arrived_ref, shift_send.at[1], shift_recv.at[1], ring.shifted(1))
    cot_shift.start()
    act_shift.start()
    prev_ref[me] = normed(stash_ref[...], gain_ref[...])
    gates_ref[me] = dense_ref[...]
    buffers = (prev_ref, cots_ref, next_ref)
    flying = {}

    def start(t, k):
        made = []
        for d, way in enumerate((1, -1)):
            block = ring.owner(-way * k)
            ref = buffers[t].at[block]
            if k == half - 1:
                ref = ref.at[:, pl.ds(d * cut, cut)]
            made.append(
                send(ref, ref, ring_send.at[t, d, k], ring_recv.at[t, d, k], ring.device(ring.sides[d]))
            )
        flying[t, k] = made
        for copy in made:
            copy.start()

    def arrive(t, k):
        for copy in flying[t, k]:
            copy.wait_recv()

    def advance(t, k):
        if k < half:
            arrive(t, k - 1)
            start(t, k)

    tile = tile_of(units)

    def pre_activations(j):
        @pl.loop(0, units // tile)
        def _(i):
            cols = columns(i, tile)
            rows = flat(prev_ref)
            pre_gate[j, :, cols] = dot(rows, wg[j, :, cols], 1, 0)
            pre_up[j, :, cols] = dot(rows, wu[j, :, cols], 1, 0)

    def gradients(j):
        weight = gate_column(gates_ref, (owners + me) * local + j)
        sums[j] = jnp.zeros(sums.shape[1:], F32)

        @pl.loop(0, units // tile)
        def _(i):
            cols = columns(i, tile)
            plain = dot(flat(cots_ref), wd[j, cols, :], 1, 1)
            gate, up = pre_gate[j, :, cols], pre_up[j, :, cols]
            sigma = jax.nn.sigmoid(gate)
            active = gate * sigma
            hidden = active * up
            d_hidden = weight * plain
            sums[j] += jnp.sum(hidden * plain, axis=1, keepdims=True)
            gated_ref[j, :, cols] = (weight * hidden).astype(BF16)
            d_gate_ref[j, :, cols] = (d_hidden * up * sigma * (1.0 + gate * (1.0 - sigma))).astype(BF16)
            d_up_ref[j, :, cols] = (d_hidden * active).astype(BF16)

    wide = tile_of(width)

    def row_gradients(low, high):
        @pl.loop(low, high)
        def _(i):
            cols = columns(i, wide)
            total = 0.0
            for j in range(local):
                total = total + dot(d_gate_ref[j], wg[j, cols, :], 1, 1)
                total = total + dot(d_up_ref[j], wu[j, cols, :], 1, 1)
            row_ref[:, :, cols] = total.astype(BF16).reshape(owners, tokens, wide)

    start(0, 0)
    gate_copies = [
        send(dense_ref, gates_ref.at[me], gate_send.at[r - 1], gate_recv.at[r - 1], ring.device(ring.peer(r)))
        for r in range(1, owners)
    ]
    for copy in gate_copies:
        copy.start()
    cot_shift.wait()
    start(1, 0)
    act_shift.wait()
    next_ref[me] = normed(arrived_ref[...], gain_ref[...])
    for k in range(1, half):
        advance(0, k)
        if k >= 2:
            advance(1, k - 1)
    start(2, 0)
    for copy in loads:
        copy.wait()
    for copy in gate_copies:
        copy.wait()
    arrive(0, half - 1)
    pre_activations(0)
    advance(1, half - 1)
    for j in range(1, local):
        pre_activations(j)
    advance(2, 1)
    arrive(1, half - 1)
    for j in range(local):
        gradients(j)
        advance(2, 2 + j)
    steps = list(range(2 + local, half))
    row_gradients(0, width // wide // 2)
    for k in steps:
        advance(2, k)
    row_gradients(width // wide // 2, width // wide)
    lane = lax.broadcasted_iota(jnp.int32, sums.shape[1:], 1)
    total = jnp.zeros(sums.shape[1:], F32)
    for j in range(local):
        total = jnp.where(lane == j, sums[j], total)
    products_ref[...] = total.astype(BF16).reshape(products_ref.shape)
    arrive(2, half - 1)
    for t in range(3):
        for k in range(half):
            for copy in flying[t, k]:
                copy.wait_send()


ANY = pl.BlockSpec(memory_space=pl.ANY)
VMEM_LIMIT = 60 * 2**20


def gather_call(sections, owners, act, stash, cot, gain, dense, wg, wu, wd):
    tokens, width = stash.shape
    local, _, units = wg.shape
    half = owners // 2
    every = jax.ShapeDtypeStruct((owners, tokens, width), BF16)
    inner = jax.ShapeDtypeStruct((local, owners * tokens, units), BF16)
    small = jax.ShapeDtypeStruct((owners,) + dense.shape, BF16)
    return pl.pallas_call(
        functools.partial(gather_kernel, sections, owners),
        out_shape=(
            jax.ShapeDtypeStruct((tokens, width), BF16),
            every, every, every, small, inner, inner, inner, every, small,
        ),
        in_specs=[VMEM] * 5 + [ANY] * 3,
        out_specs=(VMEM,) * 10,
        scratch_shapes=[
            pltpu.VMEM(wg.shape, BF16),
            pltpu.VMEM(wu.shape, BF16),
            pltpu.VMEM(wd.shape, BF16),
            pltpu.VMEM(inner.shape, F32),
            pltpu.VMEM(inner.shape, F32),
            pltpu.VMEM((local, owners * tokens, LANES), F32),
            pltpu.SemaphoreType.DMA((2,)),
            pltpu.SemaphoreType.DMA((2,)),
            pltpu.SemaphoreType.DMA((owners - 1,)),
            pltpu.SemaphoreType.DMA((owners - 1,)),
            pltpu.SemaphoreType.DMA((3, 2, half)),
            pltpu.SemaphoreType.DMA((3, 2, half)),
            pltpu.SemaphoreType.DMA((3,)),
        ],
        compiler_params=pltpu.CompilerParams(
            collective_id=0, has_side_effects=True, vmem_limit_bytes=VMEM_LIMIT
        ),
    )(act, stash, cot, gain, dense, wg, wu, wd)


def reduce_kernel(
    sections, owners,
    row_ref, products_ref, next_ref, prev_ref, cots_ref, gates_ref,
    d_gate_ref, d_up_ref, gated_ref, wg_hbm, wu_hbm, wd_hbm,
    summed_ref, mixed_ref, returned_ref, grad_gate_hbm, grad_up_hbm, grad_down_hbm,
    wg, wu, wd, hidden_ref, part_ref,
    outgoing, arriving, small_send, small_recv, ring_send, ring_recv, weight_sem, grad_sem,
):
    parts, totals, count = (row_ref, part_ref), (summed_ref, mixed_ref), 2
    local, _, units = wg.shape
    loads = load_weights((wg_hbm, wu_hbm, wd_hbm), (wg, wu, wd), weight_sem)
    ring = Ring(sections, owners)
    me, half = ring.me, ring.half
    width = parts[0].shape[2]
    cut = width // 2
    ring.greet(False)

    def start(t, k):
        made = []
        for d, way in enumerate((1, -1)):
            block = ring.owner(way * (half - k))
            cols = pl.ds(d * cut, cut)
            if k == 0:
                src = parts[t].at[block, :, cols]
                dst = arriving.at[t, d, k, :, cols]
            else:
                src, dst = outgoing.at[t, d, k - 1], arriving.at[t, d, k]
                if k == 1:
                    rest = pl.ds((1 - d) * cut, cut)
                    src[:, rest] = parts[t][block, :, rest]
                    src[:, cols] = (
                        parts[t][block, :, cols].astype(F32)
                        + arriving[t, d, k - 1, :, cols].astype(F32)
                    ).astype(BF16)
                else:
                    src[...] = (
                        parts[t][block].astype(F32) + arriving[t, d, k - 1].astype(F32)
                    ).astype(BF16)
            made.append(
                send(src, dst, ring_send.at[t, d, k], ring_recv.at[t, d, k], ring.device(ring.sides[d]))
            )
            made[-1].start()
        flying[t, k] = made

    flying = {}
    start(0, 0)
    small = [
        send(
            products_ref.at[ring.peer(r)], returned_ref.at[me],
            small_send.at[r - 1], small_recv.at[r - 1], ring.device(ring.peer(r)),
        )
        for r in range(1, owners)
    ]
    for copy in small:
        copy.start()
    returned_ref[me] = products_ref[me]
    def advance(t, k):
        if k < half:
            for copy in flying[t, k - 1]:
                copy.wait_recv()
            start(t, k)

    def finish(t):
        for copy in flying[t, half - 1]:
            copy.wait_recv()
        totals[t][...] = (
            parts[t][me].astype(F32)
            + arriving[t, 0, half - 1].astype(F32)
            + arriving[t, 1, half - 1].astype(F32)
        )

    tile, wide = tile_of(units), tile_of(width)

    def hidden(j):
        weight = gate_column(gates_ref, me * local + j)

        @pl.loop(0, units // tile)
        def _(i):
            cols = columns(i, tile)
            rows = flat(next_ref)
            gate = dot(rows, wg[j, :, cols], 1, 0)
            up = dot(rows, wu[j, :, cols], 1, 0)
            hidden_ref[j, :, cols] = (weight * (gate * jax.nn.sigmoid(gate) * up)).astype(BF16)

    def mix(low, high):
        @pl.loop(low, high)
        def _(i):
            cols = columns(i, wide)
            total = 0.0
            for j in range(local):
                total = total + dot(hidden_ref[j], wd[j, :, cols], 1, 0)
            part_ref[:, :, cols] = total.astype(BF16).reshape(part_ref.shape[:2] + (wide,))

    grads = []

    def weight_gradient(held, out_hbm, index, j):
        rows_size = held.shape[1]
        step = tile_of(rows_size)

        @pl.loop(0, rows_size // step)
        def _(i):
            rows = columns(i, step)
            if index == 2:
                left, right = gated_ref[j, :, rows], flat(cots_ref)
            else:
                left = prev_ref[:, :, rows].reshape(-1, step)
                right = (d_gate_ref, d_up_ref)[index][j]
            held[j, rows, :] = dot(left, right, 0, 0).astype(BF16)

        copy = pltpu.make_async_copy(held.at[j], out_hbm.at[j], grad_sem.at[index, j])
        copy.start()
        grads.append(copy)

    for copy in loads:
        copy.wait()
    for j in range(local):
        hidden(j)
    advance(0, 1)
    mix(0, width // wide)
    start(1, 0)
    advance(0, 2)
    hops = []
    for k in range(1, half):
        hops += [(1, k), (0, k + 2)]
    hops = [(t, k) for t, k in hops if k < half]
    for index, (held, out) in enumerate(((wg, grad_gate_hbm), (wu, grad_up_hbm), (wd, grad_down_hbm))):
        for j in range(local):
            weight_gradient(held, out, index, j)
            if hops:
                advance(*hops.pop(0))
    for hop in hops:
        advance(*hop)
    finish(0)
    finish(1)
    for copy in grads:
        copy.wait()
    for t in range(count):
        for k in range(half):
            for copy in flying[t, k]:
                copy.wait_send()
    for copy in small:
        copy.wait()


def reduce_call(sections, owners, row, products, rows_next, prev, cots, gates, inner, weights):
    _, tokens, width = row.shape
    half = owners // 2
    total = jax.ShapeDtypeStruct((tokens, width), F32)
    return pl.pallas_call(
        functools.partial(reduce_kernel, sections, owners),
        out_shape=(total, total, jax.ShapeDtypeStruct(products.shape, BF16))
        + tuple(jax.ShapeDtypeStruct(w.shape, BF16) for w in weights),
        in_specs=[VMEM] * 9 + [ANY] * 3,
        out_specs=(VMEM,) * 3 + (ANY,) * 3,
        scratch_shapes=[pltpu.VMEM(w.shape, BF16) for w in weights]
        + [
            pltpu.VMEM(inner[0].shape, BF16),
            pltpu.VMEM(row.shape, BF16),
            pltpu.VMEM((2, 2, half - 1, tokens, width), BF16),
            pltpu.VMEM((2, 2, half, tokens, width), BF16),
            pltpu.SemaphoreType.DMA((owners - 1,)),
            pltpu.SemaphoreType.DMA((owners - 1,)),
            pltpu.SemaphoreType.DMA((2, 2, half)),
            pltpu.SemaphoreType.DMA((2, 2, half)),
            pltpu.SemaphoreType.DMA((3,)),
            pltpu.SemaphoreType.DMA((3, weights[0].shape[0])),
        ],
        compiler_params=pltpu.CompilerParams(
            collective_id=1, has_side_effects=True, vmem_limit_bytes=VMEM_LIMIT
        ),
    )(row, products, rows_next, prev, cots, gates, *inner, *weights)


def apply_rms_norm(rows, gain):
    values = rows.astype(F32)
    scale = lax.rsqrt(jnp.mean(values * values, axis=-1, keepdims=True) + EPS)
    unit = values * scale
    return (unit * gain).astype(BF16), unit, scale


def dense_gates(routes, gates, experts_all):
    hit = routes[:, :, None] == jnp.arange(experts_all, dtype=jnp.int32)
    return jnp.sum(jnp.where(hit, gates.astype(F32)[:, :, None], 0.0), axis=1).astype(BF16)


def per_device(
    sent_acts,
    stash,
    cotangents,
    norm_gain,
    w_gate,
    w_up,
    w_down,
    routes_next,
    gates_next,
    routes_prev,
    gates_prev,
):
    owners = lax.axis_size("expert")
    me = lax.axis_index("expert")
    gain = norm_gain[0].astype(F32)
    wg, wu, wd = w_gate[0], w_up[0], w_down[0]
    local, width, hidden_units = wg.shape
    experts_all = local * owners
    tokens = stash.shape[1]

    dense = jnp.concatenate(
        [
            dense_gates(routes_next[0], gates_next[0], experts_all),
            dense_gates(routes_prev[0], gates_prev[0], experts_all),
        ],
        axis=1,
    )
    dense = jnp.pad(dense, ((0, 0), (0, LANES - dense.shape[1])))
    sections = lax.axis_size("section")
    _, unit_rows, scale = apply_rms_norm(stash[0], gain)
    weights = (wg, wu, wd)
    arrived, next_all, prev_all, cot_all, dense_all, d_gate, d_up, gated, row, products = gather_call(
        sections, owners, sent_acts[0], stash[0], cotangents[0], gain[None], dense, *weights
    )
    cot = lax.dynamic_index_in_dim(cot_all, me, 0, keepdims=False)
    summed, mixed, products_back, grad_gate, grad_up, grad_down = reduce_call(
        sections, owners, row, products, next_all, prev_all, cot_all, dense_all,
        (d_gate, d_up, gated), weights,
    )
    products_back = products_back[:, :, :local]

    fwd_out = (arrived.astype(F32) + mixed).astype(BF16)

    by_expert = jnp.transpose(products_back, (1, 0, 2)).reshape(tokens, experts_all).astype(F32)
    hit = routes_prev[0][:, :, None] == jnp.arange(experts_all, dtype=jnp.int32)
    gate_grad = jnp.sum(jnp.where(hit, by_expert[:, None, :], 0.0), axis=-1).astype(BF16)

    normalized_gradient = summed * gain
    backward = cot.astype(F32) + scale * (
        normalized_gradient
        - unit_rows * jnp.mean(normalized_gradient * unit_rows, axis=-1, keepdims=True)
    )
    return (
        fwd_out[None],
        backward.astype(BF16)[None],
        gate_grad[None],
        grad_gate[None],
        grad_up[None],
        grad_down[None],
    )


def solution(mesh):
    tokens = P("section", "expert", None)
    weights = P("section", "expert", None, None)
    return jax.shard_map(
        per_device,
        mesh=mesh,
        in_specs=(tokens, tokens, tokens, P("section", None), weights, weights, weights)
        + (tokens,) * 4,
        out_specs=(tokens, tokens, tokens, weights, weights, weights),
        check_vma=False,
    )
```
